32 devices in a mesh: groups: 2 (over y), wide: 4 (over z), narrow: 4 (over x, core).
Axes of the slice: x: 2, y: 2, z: 4, core: 2. Of those that a mesh axis runs over, the one named last changes fastest.
Arguments:
- tokens: bfloat16 [128, 8192], P(('groups', 'wide'), 'narrow'), parts along dimension 0, may hold values from -60 to 60
- signs: int32 [128, 8192], P(('groups', 'wide'), 'narrow'), parts along dimension 0, may hold values 0 or 1
- magnitude: float32 [128, 8192], P(('groups', 'wide'), 'narrow'), parts along dimension 0, may hold values from 0.05 to 0.5
- target: bfloat16 [128, 8192], P(('groups', 'wide'), 'narrow'), parts along dimension 0, may hold values from -6 to 6
- norm_gain: float32 [8192], P('narrow'), may hold values from 0.1 to 1.9
- gate_weight: bfloat16 [8192, 20480], P('narrow', 'wide'), may hold values from -0.0625 to 0.0625
- up_weight: bfloat16 [8192, 20480], P('narrow', 'wide'), may hold values from -0.0625 to 0.0625
- down_weight: bfloat16 [20480, 8192], P('wide', 'narrow'), may hold values from -0.0390625 to 0.0390625
Outputs:
- new_delta: float32 [128, 8192], P(('groups', 'wide'), 'narrow'), parts along dimension 0
The draws below stay inside these ranges and needn't reach their ends.
There are 2 independent parts, one for each index of `groups`. The reference program is written for one: setup_inputs(seed, part) draws one part's arguments, and reference() takes and returns one part's arrays. A program takes and returns all parts, laid end to end along the dimension named above; an argument that names none is the same for every part. Nothing has to cross between parts.
All inputs are finite; a program needn't handle non-finite values. No bound on the sum of `signs` on one device may be relied on, other than what follows from the above.
Results may differ from the reference program's by a relative error of at most 0.0034.
Values may be sent and summed in bfloat16 or wider, within the bound.
A program may use at most 192 MiB of HBM per device.

```python
import math
import jax
import jax.numpy as jnp
from jax import lax

D = 8192
FF = 20480
TOKENS = 64


def draw_tokens(key, part):
    keys = jax.random.split(jax.random.fold_in(key, 17), 3)
    pos = jnp.arange(D, dtype=jnp.float32) / D
    col_scale = 0.3 * jnp.exp(math.log(10.0) * (0.6 * pos + 0.4 * jax.random.uniform(keys[1], (D,))))
    row_scale = jnp.exp(jax.random.uniform(keys[0], (TOKENS, 1), minval=math.log(0.3), maxval=math.log(3.0)))
    base = jax.random.normal(keys[2], (TOKENS, D))
    values = jnp.clip(base * row_scale * col_scale, -60.0, 60.0)
    return values.astype(jnp.bfloat16)


def place_ends(entries, stream_key, low, top_value):
    longest = entries.shape.index(max(entries.shape))
    spots = []
    for shift in (0, 1):
        where = [jax.random.randint(jax.random.fold_in(stream_key, axis), (), 0, length) for axis, length in enumerate(entries.shape)]
        where[longest] = (where[longest] + shift) % entries.shape[longest]
        spots.append(tuple(where))
    return entries.at[spots[0]].set(low).at[spots[1]].set(top_value)


def level_of(key, extent, cuts, low, high):
    def one(position, shards_of):
        draws = jax.random.uniform(jax.random.fold_in(jax.random.fold_in(key, 6), position), (shards_of,), jnp.float32, low / len(cuts), high / len(cuts))
        return jnp.repeat(jnp.exp(draws), extent[position] // shards_of).reshape((-1,) + (1,) * (len(extent) - position - 1))

    gain = one(*cuts[0])
    for cut in cuts[1:]:
        gain = gain * one(*cut)
    return gain


def scatter_about(own_key, extent, deviation, most, cuts=(), held_as=jnp.bfloat16):
    level = level_of(own_key, extent, cuts, -0.22, 0.18) if cuts else 1.0
    drawn = jax.random.normal(own_key, extent, jnp.float32) * deviation * level
    return jnp.minimum(jnp.maximum(drawn, -most), most).astype(held_as)


def setup_inputs(seed: int = 0, part: int = 0) -> dict:
    arg_keys = jax.random.split(jax.random.key(seed), 9)
    part_splits = jax.random.split(jax.random.fold_in(arg_keys[8], part), 9)
    return {
        "tokens": draw_tokens(jax.random.fold_in(jax.random.fold_in(arg_keys[8], part), 71), part),
        "signs": place_ends((jax.random.randint(part_splits[1], (TOKENS, D), 0, 2) < 1).astype(jnp.int32), jax.random.fold_in(part_splits[1], 1), 0, 1),
        "magnitude": jnp.clip(jnp.exp(math.log(0.5) - 2.3025851 * jax.random.uniform(part_splits[2], (TOKENS, D), jnp.float32) ** level_of(part_splits[2], (TOKENS, D), ((0, 4), (1, 4)), -0.2, 0.2)), 0.05, 0.5),
        "target": scatter_about(part_splits[3], (TOKENS, D), 1.0, 6.0, ((0, 4), (1, 4))),
        "norm_gain": jnp.clip(1.0 + 0.18 * jax.random.normal(arg_keys[4], (D,), jnp.float32), 0.1, 1.9),
        "gate_weight": scatter_about(arg_keys[5], (D, FF), D ** -0.5, 0.0625, ((0, 4), (1, 4))),
        "up_weight": scatter_about(arg_keys[6], (D, FF), D ** -0.5, 0.0625, ((0, 4), (1, 4))),
        "down_weight": scatter_about(arg_keys[7], (FF, D), FF ** -0.5, 0.0390625, ((0, 4), (1, 4))),
    }


EPS = 1e-05
ASCENT = 0.5

def reference(tokens, signs, magnitude, target, norm_gain, gate_weight, up_weight, down_weight):
    delta = (2 * signs - 1).astype(jnp.float32) * magnitude
    latent = tokens.astype(jnp.float32) + delta
    scale = lax.rsqrt(lax.optimization_barrier(jnp.mean(latent * latent, axis=1, keepdims=True)) + EPS)
    unit = latent * scale
    normed = (unit * norm_gain).astype(jnp.bfloat16)
    gate = jnp.dot(normed, gate_weight, preferred_element_type=jnp.float32)
    up = jnp.dot(normed, up_weight, preferred_element_type=jnp.float32)
    back_hidden = jnp.dot(target, jnp.transpose(down_weight), preferred_element_type=jnp.float32)
    sig = jax.nn.sigmoid(gate)
    back_gate = (back_hidden * up * sig * (1.0 + gate * (1.0 - sig))).astype(jnp.bfloat16)
    back_up = (back_hidden * gate * sig).astype(jnp.bfloat16)
    back_normed = jnp.dot(back_gate, jnp.transpose(gate_weight), preferred_element_type=jnp.float32)
    back_normed = back_normed + jnp.dot(back_up, jnp.transpose(up_weight), preferred_element_type=jnp.float32)
    scaled = back_normed * norm_gain
    inner = lax.optimization_barrier(jnp.mean(scaled * unit, axis=1, keepdims=True))
    back_latent = scale * (scaled - unit * inner)
    return delta + ASCENT * (target.astype(jnp.float32) + back_latent)
```

```python
import functools
import jax
import jax.numpy as jnp
from jax import lax
from jax.experimental import pallas as pl
from jax.experimental.pallas import tpu as pltpu
from jax.sharding import PartitionSpec as P

EPS = 1e-05
ASCENT = 0.5
MESH = pl.DeviceIdType.MESH
BF = jnp.bfloat16
F32 = jnp.float32
NT = (((1,), (1,)), ((), ()))


def remote(src, dst, send_sem, recv_sem, axis, index):
    return pltpu.make_async_remote_copy(
        src_ref=src, dst_ref=dst, send_sem=send_sem, recv_sem=recv_sem,
        device_id={axis: index}, device_id_type=MESH,
    )


def plan(hidden):
    for chunks in (5, 4, 3, 2):
        if hidden % (chunks * 128) == 0:
            return chunks, hidden // chunks
    return 1, hidden


def kernel(
    dims, tok, sig, mag, tgt, gain, wg, wu, wd, out,
    wg_v, wu_v, wd_v, tg_all, xg_all, part, sq_s, sq_r, sc_own,
    a_cs, a_cr, a_own, a_xs, a_xr, b_cs, b_cr, b_own, b_xs, b_xr,
    bgu, in_all, in_r, acc, fs, fr,
    w_sem, d_sem, tg_ss, tg_rs, xg_ss, xg_rs, sq_ss, sq_rs,
    ac_ss, ac_rs, ax_ss, ax_rs, bc_ss, bc_rs, bx_ss, bx_rs,
    gx_ss, gx_rs, gc_ss, gc_rs, in_ss, in_rs, iw_ss, iw_rs, f_ss, f_rs,
):
    NW, X, C, chunks, hc, slots, pieces = dims
    nn = X * C
    Lt, Dl = tok.shape
    T = Lt * NW
    H = T // C
    R = T // nn
    D = Dl * nn
    w = lax.axis_index("wide")
    n = lax.axis_index("narrow")
    x, c = n // C, lax.rem(n, C)
    pc = lax.rem(c + 1, C)
    partner = x * C + pc
    block = c * X + x
    ctile = next(t for t in (512, 256, 128) if hc % t == 0)
    dtile = next(t for t in (512, 256, 128) if (Dl // pieces) % t == 0)
    sent = []

    def rows(i, size):
        return pl.ds(pl.multiple_of(i * size, size), size)

    def down_copy(k):
        return pltpu.make_async_copy(wd.at[pl.ds(k * hc, hc), :], wd_v.at[k % slots], d_sem.at[k % slots])

    def gu_copies(k):
        return (
            pltpu.make_async_copy(wg.at[:, pl.ds(k * hc, hc)], wg_v.at[k], w_sem.at[2 * k]),
            pltpu.make_async_copy(wu.at[:, pl.ds(k * hc, hc)], wu_v.at[k], w_sem.at[2 * k + 1]),
        )

    def go(cp):
        cp.start()
        sent.append(cp)

    for k in range(min(slots, chunks)):
        down_copy(k).start()
    for k in range(min(2, chunks)):
        for cp in gu_copies(k):
            cp.start()

    barrier = pltpu.get_barrier_semaphore()
    for k in range(1, NW):
        pl.semaphore_signal(barrier, inc=1, device_id={"wide": lax.rem(w + k, NW)}, device_id_type=MESH)
    for k in range(1, nn):
        pl.semaphore_signal(barrier, inc=1, device_id={"narrow": lax.rem(n + k, nn)}, device_id_type=MESH)
    pl.semaphore_wait(barrier, NW - 1 + nn - 1)

    mine = rows(w, Lt)
    for k in range(1, NW):
        go(remote(tgt, tg_all.at[mine], tg_ss.at[k - 1], tg_rs.at[k - 1], "wide", lax.rem(w + k, NW)))
    tg_all[mine, :] = tgt[...]
    latent = tok[...].astype(F32) + (2 * sig[...] - 1).astype(F32) * mag[...]
    sq_s[...] = jnp.broadcast_to(jnp.sum(latent * latent, axis=1, keepdims=True), (Lt, 128))
    for k in range(1, nn):
        go(remote(sq_s, sq_r.at[k - 1], sq_ss.at[k - 1], sq_rs.at[k - 1], "narrow", lax.rem(n + k, nn)))
    total = sq_s[...]
    for k in range(1, nn):
        remote(sq_s, sq_r.at[k - 1], sq_ss.at[k - 1], sq_rs.at[k - 1], "narrow", lax.rem(n + k, nn)).wait_recv()
        total = total + sq_r[k - 1]
    sc_own[...] = lax.rsqrt(total / D + EPS)
    latent = tok[...].astype(F32) + (2 * sig[...] - 1).astype(F32) * mag[...]
    xg_all[mine, :] = (latent * sc_own[...][:, :1] * gain[...]).astype(BF)
    for k in range(1, NW):
        go(remote(xg_all.at[mine], xg_all.at[mine], xg_ss.at[k - 1], xg_rs.at[k - 1], "wide", lax.rem(w + k, NW)))

    def wait_rows(dst, ss, rs, k):
        where = rows(lax.rem(w - k + NW, NW), Lt)
        remote(dst.at[where], dst.at[where], ss.at[k - 1], rs.at[k - 1], "wide", lax.rem(w + k, NW)).wait_recv()

    def stage1(k, width, cs, own, ss, rs, cr):
        own[k] = part[rows(c, H), pl.ds(0, width)]
        if C > 1:
            cs[k] = part[rows(pc, H), pl.ds(0, width)]
            go(remote(cs.at[k], cr.at[k], ss.at[k], rs.at[k], "narrow", partner))

    def stage2(k, cs, cr, own, css, crs, xs, xr, xss, xrs):
        if C > 1:
            remote(cs.at[k], cr.at[k], css.at[k], crs.at[k], "narrow", partner).wait_recv()
            own[k] = own[k] + cr[k]
        for j in range(1, X):
            to = lax.rem(x + j, X)
            xs[k, j - 1] = own[k, rows(to, R), :].astype(BF)
            s = k * (X - 1) + j - 1
            go(remote(xs.at[k, j - 1], xr.at[k, j - 1], xss.at[s], xrs.at[s], "narrow", to * C + c))

    def stage3(k, own, xs, xr, xss, xrs):
        for j in range(1, X):
            to = lax.rem(x + j, X)
            s = k * (X - 1) + j - 1
            remote(xs.at[k, j - 1], xr.at[k, j - 1], xss.at[s], xrs.at[s], "narrow", to * C + c).wait_recv()
        total = own[k, rows(x, R), :]
        for j in range(1, X):
            total = total + xr[k, j - 1].astype(F32)
        own[k, rows(x, R), :] = total

    brows = rows(block, R)

    def stage4(k):
        stage3(k, b_own, b_xs, b_xr, bx_ss, bx_rs)
        gate = b_own[k, rows(x, R), pl.ds(0, hc)]
        up = b_own[k, rows(x, R), pl.ds(hc, hc)]
        bh = a_own[k, rows(x, R), :]
        g = jax.nn.sigmoid(gate)
        bg = (bh * up * g * (1.0 + gate * (1.0 - g))).astype(BF)
        bu = (bh * gate * g).astype(BF)
        bgu[k, brows, pl.ds(0, hc)] = bg
        bgu[k, brows, pl.ds(hc, hc)] = bu
        got = jnp.broadcast_to(
            jnp.sum(bg.astype(F32) * gate + bu.astype(F32) * up, axis=1, keepdims=True), (R, 128)
        )
        in_all[brows, :] = got if k == 0 else in_all[brows, :] + got
        for j in range(1, X):
            q = k * (X - 1) + j - 1
            go(remote(bgu.at[k, brows], bgu.at[k, brows], gx_ss.at[q], gx_rs.at[q], "narrow", lax.rem(x + j, X) * C + c))
        if k == chunks - 1:
            for j in range(1, nn):
                go(remote(in_all.at[brows], in_all.at[brows], in_ss.at[j - 1], in_rs.at[j - 1], "narrow", lax.rem(n + j, nn)))

    def stage5(k):
        for j in range(1, X):
            q = k * (X - 1) + j - 1
            where = rows(c * X + lax.rem(x - j + X, X), R)
            remote(bgu.at[k, where], bgu.at[k, where], gx_ss.at[q], gx_rs.at[q], "narrow", lax.rem(x + j, X) * C + c).wait_recv()
        if C > 1:
            half = rows(c, H)
            go(remote(bgu.at[k, half], bgu.at[k, half], gc_ss.at[k], gc_rs.at[k], "narrow", partner))

    def stage6(k):
        if C > 1:
            half = rows(pc, H)
            remote(bgu.at[k, half], bgu.at[k, half], gc_ss.at[k], gc_rs.at[k], "narrow", partner).wait_recv()

    def inner_stage():
        for j in range(1, nn):
            other = lax.rem(n - j + nn, nn)
            where = rows(lax.rem(other, C) * X + other // C, R)
            remote(in_all.at[where], in_all.at[where], in_ss.at[j - 1], in_rs.at[j - 1], "narrow", lax.rem(n + j, nn)).wait_recv()
        for k in range(1, NW):
            to = lax.rem(w + k, NW)
            go(remote(in_all.at[rows(to, Lt)], in_r.at[k - 1], iw_ss.at[k - 1], iw_rs.at[k - 1], "wide", to))

    tasks = [("A", k) for k in range(chunks)] + [("B", k) for k in range(chunks)] + [("C", k) for k in range(chunks)]
    order = {t: i for i, t in enumerate(tasks)}
    after = {i: [] for i in range(len(tasks) + 4)}
    for k in range(chunks):
        i = order[("A", k)]
        after[i].append(lambda k=k: stage1(k, hc, a_cs, a_own, ac_ss, ac_rs, a_cr))
        after[i + 1].append(lambda k=k: stage2(k, a_cs, a_cr, a_own, ac_ss, ac_rs, a_xs, a_xr, ax_ss, ax_rs))
        after[i + 2].append(lambda k=k: stage3(k, a_own, a_xs, a_xr, ax_ss, ax_rs))
    for k in range(chunks):
        i = order[("B", k)]
        after[i].append(lambda k=k: stage1(k, 2 * hc, b_cs, b_own, bc_ss, bc_rs, b_cr))
        after[i + 1].append(lambda k=k: stage2(k, b_cs, b_cr, b_own, bc_ss, bc_rs, b_xs, b_xr, bx_ss, bx_rs))
        after[i + 2].append(lambda k=k: stage4(k))
        after[i + 3].append(lambda k=k: stage5(k))

    def final_send(p):
        width = Dl // pieces
        cols = pl.ds(p * width, width)
        for k in range(1, NW):
            to = lax.rem(w + k, NW)
            q = (k - 1) * pieces + p
            fs[k - 1, :, cols] = acc[rows(to, Lt), cols].astype(BF)
            go(remote(fs.at[k - 1, :, cols], fr.at[k - 1, :, cols], f_ss.at[q], f_rs.at[q], "wide", to))

    done = set()

    def run_after(i):
        if i in done:
            return
        done.add(i)
        for f in reversed(after[i]):
            f()

    for i, (kind, k) in enumerate(tasks):
        if kind == "A":
            if k == 0:
                for j in range(1, NW):
                    wait_rows(tg_all, tg_ss, tg_rs, j)
            down_copy(k).wait()
            if k + 2 < chunks:
                for cp in gu_copies(k + 2):
                    cp.start()

            @pl.loop(0, hc // ctile)
            def _(t):
                cols = rows(t, ctile)
                part[:, cols] = lax.dot_general(
                    tg_all[...], wd_v[k % slots, cols, :], NT, preferred_element_type=F32
                )

            if k + slots < chunks:
                down_copy(k + slots).start()
        elif kind == "B":
            if k == 0:
                for j in range(1, NW):
                    wait_rows(xg_all, xg_ss, xg_rs, j)
            for cp in gu_copies(k):
                cp.wait()

            @pl.loop(0, hc // ctile)
            def _(t):
                part[:, rows(t, ctile)] = jnp.dot(
                    xg_all[...], wg_v[k, :, rows(t, ctile)], preferred_element_type=F32
                )
                part[:, pl.ds(pl.multiple_of(hc + t * ctile, ctile), ctile)] = jnp.dot(
                    xg_all[...], wu_v[k, :, rows(t, ctile)], preferred_element_type=F32
                )
        else:
            for q in range(i):
                run_after(q)
            if order[("B", k)] + 3 >= i:
                for q in range(i, order[("B", k)] + 4):
                    run_after(q)
            stage6(k)
            last = k == chunks - 1
            if last:
                for q in sorted(after):
                    run_after(q)
                inner_stage()
            per = (Dl // dtile) // pieces
            for p in range(pieces if last else 1):
                lo, hi = (p * per, (p + 1) * per) if last else (0, Dl // dtile)

                @pl.loop(lo, hi)
                def _(t):
                    cols = rows(t, dtile)
                    got = lax.dot_general(
                        bgu[k, :, pl.ds(0, hc)], wg_v[k, cols, :], NT, preferred_element_type=F32
                    ) + lax.dot_general(
                        bgu[k, :, pl.ds(hc, hc)], wu_v[k, cols, :], NT, preferred_element_type=F32
                    )
                    if k == 0:
                        acc[:, cols] = got
                    else:
                        acc[:, cols] = acc[:, cols] + got

                if last:
                    final_send(p)
        run_after(i)

    inner = in_all[mine, :]
    for k in range(1, NW):
        to = lax.rem(w + k, NW)
        remote(in_all.at[rows(to, Lt)], in_r.at[k - 1], iw_ss.at[k - 1], iw_rs.at[k - 1], "wide", to).wait_recv()
        inner = inner + in_r[k - 1]
    scale = sc_own[...][:, :1]
    mean = inner[:, :1] / D
    width = Dl // pieces
    for p in range(pieces):
        cols = pl.ds(p * width, width)
        total = acc[mine, cols]
        for k in range(1, NW):
            to = lax.rem(w + k, NW)
            q = (k - 1) * pieces + p
            remote(fs.at[k - 1, :, cols], fr.at[k - 1, :, cols], f_ss.at[q], f_rs.at[q], "wide", to).wait_recv()
            total = total + fr[k - 1, :, cols].astype(F32)
        delta = (2 * sig[:, cols] - 1).astype(F32) * mag[:, cols]
        unit = (tok[:, cols].astype(F32) + delta) * scale
        back = scale * (total * gain[:, cols] - unit * mean)
        out[:, cols] = delta + ASCENT * (tgt[:, cols].astype(F32) + back)
    for cp in sent:
        cp.wait_send()


def on_device(NW, nn, tokens, signs, magnitude, target, norm_gain, gate_weight, up_weight, down_weight):
    Lt, Dl = tokens.shape
    hidden = gate_weight.shape[1]
    T = Lt * NW
    C = 2 if nn % 2 == 0 else 1
    X = nn // C
    chunks, hc = plan(hidden)
    slots = min(3, chunks)
    pieces = 4 if Dl % 512 == 0 else 1
    H, R = T // C, T // nn
    dims = (NW, X, C, chunks, hc, slots, pieces)
    V = pltpu.VMEM
    S = lambda k: pltpu.SemaphoreType.DMA((max(k, 1),))
    mw, mn, mx = NW - 1, nn - 1, X - 1
    scratch = [
        V((chunks, Dl, hc), BF), V((chunks, Dl, hc), BF), V((slots, hc, Dl), BF),
        V((T, Dl), BF), V((T, Dl), BF), V((T, 2 * hc), F32),
        V((Lt, 128), F32), V((max(mn, 1), Lt, 128), F32), V((Lt, 128), F32),
        V((chunks, H, hc), F32), V((chunks, H, hc), F32), V((chunks, H, hc), F32),
        V((chunks, max(mx, 1), R, hc), BF), V((chunks, max(mx, 1), R, hc), BF),
        V((chunks, H, 2 * hc), F32), V((chunks, H, 2 * hc), F32), V((chunks, H, 2 * hc), F32),
        V((chunks, max(mx, 1), R, 2 * hc), BF), V((chunks, max(mx, 1), R, 2 * hc), BF),
        V((chunks, T, 2 * hc), BF), V((T, 128), F32), V((max(mw, 1), Lt, 128), F32),
        V((T, Dl), F32), V((max(mw, 1), Lt, Dl), BF), V((max(mw, 1), Lt, Dl), BF),
        S(2 * chunks), S(slots),
        S(mw), S(mw), S(mw), S(mw), S(mn), S(mn),
        S(chunks), S(chunks), S(chunks * mx), S(chunks * mx),
        S(chunks), S(chunks), S(chunks * mx), S(chunks * mx),
        S(chunks * mx), S(chunks * mx), S(chunks), S(chunks),
        S(mn), S(mn), S(mw), S(mw), S(mw * pieces), S(mw * pieces),
    ]
    vm = pl.BlockSpec(memory_space=pltpu.VMEM)
    hbm = pl.BlockSpec(memory_space=pl.ANY)
    return pl.pallas_call(
        functools.partial(kernel, dims),
        out_shape=jax.ShapeDtypeStruct((Lt, Dl), F32),
        in_specs=[vm] * 5 + [hbm] * 3,
        out_specs=vm,
        scratch_shapes=scratch,
        compiler_params=pltpu.CompilerParams(
            collective_id=0, has_side_effects=True, vmem_limit_bytes=67043328
        ),
    )(tokens, signs, magnitude, target, norm_gain.reshape(1, Dl), gate_weight, up_weight, down_weight)


def solution(mesh):
    in_specs = (
        P(("groups", "wide"), "narrow"),
        P(("groups", "wide"), "narrow"),
        P(("groups", "wide"), "narrow"),
        P(("groups", "wide"), "narrow"),
        P("narrow"),
        P("narrow", "wide"),
        P("narrow", "wide"),
        P("wide", "narrow"),
    )
    return jax.shard_map(
        functools.partial(on_device, mesh.shape["wide"], mesh.shape["narrow"]),
        mesh=mesh, in_specs=in_specs, out_specs=P(("groups", "wide"), "narrow"), check_vma=False,
    )
```

```python
import functools
import jax
import jax.numpy as jnp
from jax import lax
from jax.experimental import pallas as pl
from jax.experimental.pallas import tpu as pltpu
from jax.sharding import PartitionSpec as P

EPS = 1e-05
ASCENT = 0.5
MESH = pl.DeviceIdType.MESH
BF = jnp.bfloat16
F32 = jnp.float32
NT = (((1,), (1,)), ((), ()))


def remote(src, dst, send_sem, recv_sem, axis, index):
    return pltpu.make_async_remote_copy(
        src_ref=src, dst_ref=dst, send_sem=send_sem, recv_sem=recv_sem,
        device_id={axis: index}, device_id_type=MESH,
    )


def plan(hidden):
    for chunks in (5, 4, 3, 2):
        if hidden % (chunks * 128) == 0:
            return chunks, hidden // chunks
    return 1, hidden


def kernel(
    dims, tok, sig, mag, tgt, gain, wg, wu, wd, out,
    wg_v, wu_v, wd_v, tg_all, xg_all, part, sq_s, sq_r, sc_own,
    a_cs, a_cr, a_own, a_xs, a_xr, b_cs, b_cr, b_own, b_xs, b_xr,
    bgu, in_all, in_r, acc, fs, fr, in_s, iy_r, ys, yr,
    w_sem, d_sem, tg_ss, tg_rs, xg_ss, xg_rs, sq_ss, sq_rs,
    ac_ss, ac_rs, ax_ss, ax_rs, bc_ss, bc_rs, bx_ss, bx_rs,
    gx_ss, gx_rs, gc_ss, gc_rs, in_ss, in_rs, iw_ss, iw_rs, f_ss, f_rs,
    ty_ss, ty_rs, xy_ss, xy_rs, iy_ss, iy_rs, y_ss, y_rs,
):
    G, NW, X, C, chunks, hc, slots, ahead, pieces = dims
    nn = X * C
    Lt, Dl = tok.shape
    T = Lt * NW * G
    H = T // C
    R = T // nn
    D = Dl * nn
    w = lax.axis_index("wide")
    g = lax.axis_index("groups") if G > 1 else 0
    own_w = g * NW + w
    base = g * (chunks * hc)
    n = lax.axis_index("narrow")
    x, c = n // C, lax.rem(n, C)
    pc = lax.rem(c + 1, C)
    partner = x * C + pc
    block = c * X + x
    ctile = next(t for t in (512, 256, 128) if hc % t == 0)
    dtile = next(t for t in (512, 256, 128) if (Dl // pieces) % t == 0)
    sent = []

    def rows(i, size):
        return pl.ds(pl.multiple_of(i * size, size), size)

    def hidden_cols(k):
        return pl.ds(pl.multiple_of(base + k * hc, 128), hc)

    def down_copy(k):
        return pltpu.make_async_copy(wd.at[hidden_cols(k), :], wd_v.at[k % slots], d_sem.at[k % slots])

    def gu_copies(k):
        return (
            pltpu.make_async_copy(wg.at[:, hidden_cols(k)], wg_v.at[k], w_sem.at[2 * k]),
            pltpu.make_async_copy(wu.at[:, hidden_cols(k)], wu_v.at[k], w_sem.at[2 * k + 1]),
        )

    def go(cp):
        cp.start()
        sent.append(cp)

    for k in range(min(slots, chunks)):
        down_copy(k).start()
    for k in range(min(ahead, chunks)):
        for cp in gu_copies(k):
            cp.start()

    barrier = pltpu.get_barrier_semaphore()
    for k in range(1, NW):
        pl.semaphore_signal(barrier, inc=1, device_id={"wide": lax.rem(w + k, NW)}, device_id_type=MESH)
    for k in range(1, nn):
        pl.semaphore_signal(barrier, inc=1, device_id={"narrow": lax.rem(n + k, nn)}, device_id_type=MESH)
    for k in range(1, G):
        pl.semaphore_signal(barrier, inc=1, device_id={"groups": lax.rem(g + k, G)}, device_id_type=MESH)
    pl.semaphore_wait(barrier, NW - 1 + nn - 1 + G - 1)

    mine = rows(own_w, Lt)

    def share(src, dst, k, ss, rs):
        where = rows(g * NW + lax.rem(w - k + NW, NW), Lt)
        for j in range(1, G):
            q = (j - 1) * NW + k
            go(remote(src if k == 0 else dst.at[where], dst.at[where], ss.at[q], rs.at[q], "groups", lax.rem(g + j, G)))

    def wait_shared(dst, ss, rs):
        for k in range(NW):
            for j in range(1, G):
                q = (j - 1) * NW + k
                where = rows(lax.rem(g - j + G, G) * NW + lax.rem(w - k + NW, NW), Lt)
                remote(dst.at[where], dst.at[where], ss.at[q], rs.at[q], "groups", lax.rem(g + j, G)).wait_recv()

    for k in range(1, NW):
        go(remote(tgt, tg_all.at[mine], tg_ss.at[k - 1], tg_rs.at[k - 1], "wide", lax.rem(w + k, NW)))
    share(tgt, tg_all, 0, ty_ss, ty_rs)
    tg_all[mine, :] = tgt[...]
    latent = tok[...].astype(F32) + (2 * sig[...] - 1).astype(F32) * mag[...]
    sq_s[...] = jnp.broadcast_to(jnp.sum(latent * latent, axis=1, keepdims=True), (Lt, 128))
    for k in range(1, nn):
        go(remote(sq_s, sq_r.at[k - 1], sq_ss.at[k - 1], sq_rs.at[k - 1], "narrow", lax.rem(n + k, nn)))
    total = sq_s[...]
    for k in range(1, nn):
        remote(sq_s, sq_r.at[k - 1], sq_ss.at[k - 1], sq_rs.at[k - 1], "narrow", lax.rem(n + k, nn)).wait_recv()
        total = total + sq_r[k - 1]
    sc_own[...] = lax.rsqrt(total / D + EPS)
    latent = tok[...].astype(F32) + (2 * sig[...] - 1).astype(F32) * mag[...]
    xg_all[mine, :] = (latent * sc_own[...][:, :1] * gain[...]).astype(BF)
    for k in range(1, NW):
        go(remote(xg_all.at[mine], xg_all.at[mine], xg_ss.at[k - 1], xg_rs.at[k - 1], "wide", lax.rem(w + k, NW)))
    share(xg_all.at[mine], xg_all, 0, xy_ss, xy_rs)

    def wait_rows(dst, ss, rs, k):
        where = rows(g * NW + lax.rem(w - k + NW, NW), Lt)
        remote(dst.at[where], dst.at[where], ss.at[k - 1], rs.at[k - 1], "wide", lax.rem(w + k, NW)).wait_recv()

    def stage1(k, width, cs, own, ss, rs, cr):
        own[k] = part[rows(c, H), pl.ds(0, width)]
        if C > 1:
            cs[k] = part[rows(pc, H), pl.ds(0, width)]
            go(remote(cs.at[k], cr.at[k], ss.at[k], rs.at[k], "narrow", partner))

    def stage2(k, cs, cr, own, css, crs, xs, xr, xss, xrs):
        if C > 1:
            remote(cs.at[k], cr.at[k], css.at[k], crs.at[k], "narrow", partner).wait_recv()
            own[k] = own[k] + cr[k]
        for j in range(1, X):
            to = lax.rem(x + j, X)
            xs[k, j - 1] = own[k, rows(to, R), :].astype(BF)
            s = k * (X - 1) + j - 1
            go(remote(xs.at[k, j - 1], xr.at[k, j - 1], xss.at[s], xrs.at[s], "narrow", to * C + c))

    def stage3(k, own, xs, xr, xss, xrs):
        for j in range(1, X):
            to = lax.rem(x + j, X)
            s = k * (X - 1) + j - 1
            remote(xs.at[k, j - 1], xr.at[k, j - 1], xss.at[s], xrs.at[s], "narrow", to * C + c).wait_recv()
        total = own[k, rows(x, R), :]
        for j in range(1, X):
            total = total + xr[k, j - 1].astype(F32)
        own[k, rows(x, R), :] = total

    brows = rows(block, R)

    def stage4(k):
        stage3(k, b_own, b_xs, b_xr, bx_ss, bx_rs)
        gate = b_own[k, rows(x, R), pl.ds(0, hc)]
        up = b_own[k, rows(x, R), pl.ds(hc, hc)]
        bh = a_own[k, rows(x, R), :]
        g = jax.nn.sigmoid(gate)
        bg = (bh * up * g * (1.0 + gate * (1.0 - g))).astype(BF)
        bu = (bh * gate * g).astype(BF)
        bgu[k, brows, pl.ds(0, hc)] = bg
        bgu[k, brows, pl.ds(hc, hc)] = bu
        got = jnp.broadcast_to(
            jnp.sum(bg.astype(F32) * gate + bu.astype(F32) * up, axis=1, keepdims=True), (R, 128)
        )
        in_all[brows, :] = got if k == 0 else in_all[brows, :] + got
        for j in range(1, X):
            q = k * (X - 1) + j - 1
            go(remote(bgu.at[k, brows], bgu.at[k, brows], gx_ss.at[q], gx_rs.at[q], "narrow", lax.rem(x + j, X) * C + c))
        if k == chunks - 1:
            for j in range(1, nn):
                go(remote(in_all.at[brows], in_all.at[brows], in_ss.at[j - 1], in_rs.at[j - 1], "narrow", lax.rem(n + j, nn)))

    def stage5(k):
        for j in range(1, X):
            q = k * (X - 1) + j - 1
            where = rows(c * X + lax.rem(x - j + X, X), R)
            remote(bgu.at[k, where], bgu.at[k, where], gx_ss.at[q], gx_rs.at[q], "narrow", lax.rem(x + j, X) * C + c).wait_recv()
        if C > 1:
            half = rows(c, H)
            go(remote(bgu.at[k, half], bgu.at[k, half], gc_ss.at[k], gc_rs.at[k], "narrow", partner))

    def stage6(k):
        if C > 1:
            half = rows(pc, H)
            remote(bgu.at[k, half], bgu.at[k, half], gc_ss.at[k], gc_rs.at[k], "narrow", partner).wait_recv()

    def inner_stage():
        for j in range(1, nn):
            other = lax.rem(n - j + nn, nn)
            where = rows(lax.rem(other, C) * X + other // C, R)
            remote(in_all.at[where], in_all.at[where], in_ss.at[j - 1], in_rs.at[j - 1], "narrow", lax.rem(n + j, nn)).wait_recv()
        for j in range(1, G):
            to = lax.rem(g + j, G)
            go(remote(in_all.at[rows(to, Lt * NW)], iy_r.at[j - 1], iy_ss.at[j - 1], iy_rs.at[j - 1], "groups", to))

    def inner_wide():
        ours = rows(g, Lt * NW)
        total = in_all[ours, :]
        for j in range(1, G):
            to = lax.rem(g + j, G)
            remote(in_all.at[rows(to, Lt * NW)], iy_r.at[j - 1], iy_ss.at[j - 1], iy_rs.at[j - 1], "groups", to).wait_recv()
            total = total + iy_r[j - 1]
        in_s[...] = total
        for k in range(1, NW):
            to = lax.rem(w + k, NW)
            go(remote(in_s.at[rows(to, Lt)], in_r.at[k - 1], iw_ss.at[k - 1], iw_rs.at[k - 1], "wide", to))

    tasks = [("A", k) for k in range(chunks)] + [("B", k) for k in range(chunks)] + [("C", k) for k in range(chunks)]
    order = {t: i for i, t in enumerate(tasks)}
    after = {i: [] for i in range(len(tasks) + 4)}
    for k in range(chunks):
        i = order[("A", k)]
        after[i].append(lambda k=k: stage1(k, hc, a_cs, a_own, ac_ss, ac_rs, a_cr))
        after[i + 1].append(lambda k=k: stage2(k, a_cs, a_cr, a_own, ac_ss, ac_rs, a_xs, a_xr, ax_ss, ax_rs))
        after[i + 2].append(lambda k=k: stage3(k, a_own, a_xs, a_xr, ax_ss, ax_rs))
    for k in range(chunks):
        i = order[("B", k)]
        after[i].append(lambda k=k: stage1(k, 2 * hc, b_cs, b_own, bc_ss, bc_rs, b_cr))
        after[i + 1].append(lambda k=k: stage2(k, b_cs, b_cr, b_own, bc_ss, bc_rs, b_xs, b_xr, bx_ss, bx_rs))
        after[i + 2].append(lambda k=k: stage4(k))
        after[i + 3].append(lambda k=k: stage5(k))

    def final_groups(p):
        width = Dl // pieces
        cols = pl.ds(p * width, width)
        for j in range(1, G):
            to = lax.rem(g + j, G)
            q = (j - 1) * pieces + p
            ys[j - 1, :, cols] = acc[rows(to, Lt * NW), cols].astype(BF)
            go(remote(ys.at[j - 1, :, cols], yr.at[j - 1, :, cols], y_ss.at[q], y_rs.at[q], "groups", to))

    def final_send(p):
        width = Dl // pieces
        cols = pl.ds(p * width, width)
        ours = rows(g, Lt * NW)
        for j in range(1, G):
            to = lax.rem(g + j, G)
            q = (j - 1) * pieces + p
            remote(ys.at[j - 1, :, cols], yr.at[j - 1, :, cols], y_ss.at[q], y_rs.at[q], "groups", to).wait_recv()
            acc[ours, cols] = acc[ours, cols] + yr[j - 1, :, cols].astype(F32)
        for k in range(1, NW):
            to = lax.rem(w + k, NW)
            q = (k - 1) * pieces + p
            fs[k - 1, :, cols] = acc[rows(g * NW + to, Lt), cols].astype(BF)
            go(remote(fs.at[k - 1, :, cols], fr.at[k - 1, :, cols], f_ss.at[q], f_rs.at[q], "wide", to))

    done = set()

    def run_after(i):
        if i in done:
            return
        done.add(i)
        for f in reversed(after[i]):
            f()

    for i, (kind, k) in enumerate(tasks):
        if kind == "A":
            if k == 0:
                for j in range(1, NW):
                    wait_rows(tg_all, tg_ss, tg_rs, j)
                    share(None, tg_all, j, ty_ss, ty_rs)
                wait_shared(tg_all, ty_ss, ty_rs)
            down_copy(k).wait()
            if k + ahead < chunks:
                for cp in gu_copies(k + ahead):
                    cp.start()

            @pl.loop(0, hc // ctile)
            def _(t):
                cols = rows(t, ctile)
                part[:, cols] = lax.dot_general(
                    tg_all[...], wd_v[k % slots, cols, :], NT, preferred_element_type=F32
                )

            if k + slots < chunks:
                down_copy(k + slots).start()
            if k == 0:
                for j in range(1, NW):
                    wait_rows(xg_all, xg_ss, xg_rs, j)
                    share(None, xg_all, j, xy_ss, xy_rs)
        elif kind == "B":
            if k == 0:
                wait_shared(xg_all, xy_ss, xy_rs)
            for cp in gu_copies(k):
                cp.wait()

            @pl.loop(0, hc // ctile)
            def _(t):
                part[:, rows(t, ctile)] = jnp.dot(
                    xg_all[...], wg_v[k, :, rows(t, ctile)], preferred_element_type=F32
                )
                part[:, pl.ds(pl.multiple_of(hc + t * ctile, ctile), ctile)] = jnp.dot(
                    xg_all[...], wu_v[k, :, rows(t, ctile)], preferred_element_type=F32
                )
        else:
            for q in range(i):
                run_after(q)
            if order[("B", k)] + 3 >= i:
                for q in range(i, order[("B", k)] + 4):
                    run_after(q)
            stage6(k)
            last = k == chunks - 1
            if last:
                for q in sorted(after):
                    run_after(q)
                inner_stage()
            per = (Dl // dtile) // pieces
            for p in range(pieces if last else 1):
                lo, hi = (p * per, (p + 1) * per) if last else (0, Dl // dtile)

                @pl.loop(lo, hi)
                def _(t):
                    cols = rows(t, dtile)
                    got = lax.dot_general(
                        bgu[k, :, pl.ds(0, hc)], wg_v[k, cols, :], NT, preferred_element_type=F32
                    ) + lax.dot_general(
                        bgu[k, :, pl.ds(hc, hc)], wu_v[k, cols, :], NT, preferred_element_type=F32
                    )
                    if k == 0:
                        acc[:, cols] = got
                    else:
                        acc[:, cols] = acc[:, cols] + got

                if last:
                    final_groups(p)
                    if p > 0:
                        final_send(p - 1)
            if last:
                final_send(pieces - 1)
                inner_wide()
        run_after(i)

    inner = in_s[rows(w, Lt), :]
    for k in range(1, NW):
        to = lax.rem(w + k, NW)
        remote(in_s.at[rows(to, Lt)], in_r.at[k - 1], iw_ss.at[k - 1], iw_rs.at[k - 1], "wide", to).wait_recv()
        inner = inner + in_r[k - 1]
    scale = sc_own[...][:, :1]
    mean = inner[:, :1] / D
    width = Dl // pieces
    for p in range(pieces):
        cols = pl.ds(p * width, width)
        total = acc[mine, cols]
        for k in range(1, NW):
            to = lax.rem(w + k, NW)
            q = (k - 1) * pieces + p
            remote(fs.at[k - 1, :, cols], fr.at[k - 1, :, cols], f_ss.at[q], f_rs.at[q], "wide", to).wait_recv()
            total = total + fr[k - 1, :, cols].astype(F32)
        delta = (2 * sig[:, cols] - 1).astype(F32) * mag[:, cols]
        unit = (tok[:, cols].astype(F32) + delta) * scale
        back = scale * (total * gain[:, cols] - unit * mean)
        out[:, cols] = delta + ASCENT * (tgt[:, cols].astype(F32) + back)
    for cp in sent:
        cp.wait_send()


def on_device(groups, NW, nn, tokens, signs, magnitude, target, norm_gain, gate_weight, up_weight, down_weight):
    Lt, Dl = tokens.shape
    hidden = gate_weight.shape[1]
    G = groups if hidden % (groups * 128) == 0 else 1
    T = Lt * NW * G
    C = 2 if nn % 2 == 0 else 1
    X = nn // C
    chunks, hc = plan(hidden // G)
    slots = chunks if G > 1 else min(3, chunks)
    ahead = chunks if G > 1 else 2
    pieces = 4 if Dl % 512 == 0 else 1
    H, R = T // C, T // nn
    dims = (G, NW, X, C, chunks, hc, slots, ahead, pieces)
    V = pltpu.VMEM
    S = lambda k: pltpu.SemaphoreType.DMA((max(k, 1),))
    mw, mn, mx = NW - 1, nn - 1, X - 1
    scratch = [
        V((chunks, Dl, hc), BF), V((chunks, Dl, hc), BF), V((slots, hc, Dl), BF),
        V((T, Dl), BF), V((T, Dl), BF), V((T, 2 * hc), F32),
        V((Lt, 128), F32), V((max(mn, 1), Lt, 128), F32), V((Lt, 128), F32),
        V((chunks, H, hc), F32), V((chunks, H, hc), F32), V((chunks, H, hc), F32),
        V((chunks, max(mx, 1), R, hc), BF), V((chunks, max(mx, 1), R, hc), BF),
        V((chunks, H, 2 * hc), F32), V((chunks, H, 2 * hc), F32), V((chunks, H, 2 * hc), F32),
        V((chunks, max(mx, 1), R, 2 * hc), BF), V((chunks, max(mx, 1), R, 2 * hc), BF),
        V((chunks, T, 2 * hc), BF), V((T, 128), F32), V((max(mw, 1), Lt, 128), F32),
        V((T, Dl), F32), V((max(mw, 1), Lt, Dl), BF), V((max(mw, 1), Lt, Dl), BF),
        V((Lt * NW, 128), F32), V((max(G - 1, 1), Lt * NW, 128), F32),
        V((max(G - 1, 1), Lt * NW, Dl), BF), V((max(G - 1, 1), Lt * NW, Dl), BF),
        S(2 * chunks), S(slots),
        S(mw), S(mw), S(mw), S(mw), S(mn), S(mn),
        S(chunks), S(chunks), S(chunks * mx), S(chunks * mx),
        S(chunks), S(chunks), S(chunks * mx), S(chunks * mx),
        S(chunks * mx), S(chunks * mx), S(chunks), S(chunks),
        S(mn), S(mn), S(mw), S(mw), S(mw * pieces), S(mw * pieces),
        S((G - 1) * NW), S((G - 1) * NW), S((G - 1) * NW), S((G - 1) * NW),
        S(G - 1), S(G - 1), S((G - 1) * pieces), S((G - 1) * pieces),
    ]
    vm = pl.BlockSpec(memory_space=pltpu.VMEM)
    hbm = pl.BlockSpec(memory_space=pl.ANY)
    return pl.pallas_call(
        functools.partial(kernel, dims),
        out_shape=jax.ShapeDtypeStruct((Lt, Dl), F32),
        in_specs=[vm] * 5 + [hbm] * 3,
        out_specs=vm,
        scratch_shapes=scratch,
        compiler_params=pltpu.CompilerParams(
            collective_id=0, has_side_effects=True, vmem_limit_bytes=67043328
        ),
    )(tokens, signs, magnitude, target, norm_gain.reshape(1, Dl), gate_weight, up_weight, down_weight)


def solution(mesh):
    in_specs = (
        P(("groups", "wide"), "narrow"),
        P(("groups", "wide"), "narrow"),
        P(("groups", "wide"), "narrow"),
        P(("groups", "wide"), "narrow"),
        P("narrow"),
        P("narrow", "wide"),
        P("narrow", "wide"),
        P("wide", "narrow"),
    )
    return jax.shard_map(
        functools.partial(on_device, mesh.shape["groups"], mesh.shape["wide"], mesh.shape["narrow"]),
        mesh=mesh, in_specs=in_specs, out_specs=P(("groups", "wide"), "narrow"), check_vma=False,
    )
```
